256 devices in a mesh: kv: 2 (over core), seq: 128 (over z, y, x).
Axes of the slice: x: 4, y: 4, z: 8, core: 2. Of those that a mesh axis runs over, the one named last changes fastest.
Arguments:
- tokens: bfloat16 [32768, 4096], P(('seq', 'kv')), may hold values from -6 to 6
- gain: float32 [4096], replicated, may hold values from 0.25 to 1.75
- w_query: bfloat16 [4096, 4096], P(None, 'kv'), may hold values from -1 to 1
- w_key: bfloat16 [4096, 1024], P(None, 'kv'), may hold values from -4 to 4
- w_value: bfloat16 [4096, 1024], P(None, 'kv'), may hold values from -0.09375 to 0.09375
- w_out: bfloat16 [4096, 4096], P('kv'), may hold values from -0.09375 to 0.09375
- segment_ids: int32 [32768], replicated, may hold values from 0 to 32767, as said below
- page_table: int32 [256], P('seq'), may hold values from 0 to 1, as said below
Outputs:
- mixed: bfloat16 [32768, 4096], P(('seq', 'kv'))
- attn_out: bfloat16 [32768, 4096], P(('seq', 'kv'))
- page_pool: bfloat16 [256, 2, 8, 128, 128], P('seq', None, 'kv')
The draws below stay inside these ranges and needn't reach their ends.
Inputs may be any that keep to these rules, and one draw needn't show every extreme that they name: `segment_ids`: never falls along the stream; tokens of one prompt share the position of its first token as id; every prompt has 1 to 2048 tokens; exactly two prompts have 2048 tokens, one in each half of the stream, each beginning inside a block of 256 tokens and not at its first token; every other prompt has fewer than 128 tokens; the last token of the stream is a prompt of its own. `page_table`: in each aligned block of 2 entries every value appears once.
All inputs are finite; a program needn't handle non-finite values.
Results may differ from the reference program's by a relative error of at most 0.0065.
The reference program's roundings to bfloat16 on the way (of `normed`, `query`, `key_rows`, `value_rows`, `weights` and `attention`) count: a program that leaves them out, or rounds other values in their place, can miss the bound.
Values may be sent and summed in bfloat16 or wider, within the bound.
A program may use at most 192 MiB of HBM per device.

```python
import jax
import jax.numpy as jnp
from jax import lax

D = 4096
HEADS = 32
KVH = 8
HD = 128
PAGE = 128
SHORT = 64
BLOCK = 256
TOKENS = 32768
REACH = 8
LONGSEG = 2048
PAGES = 256
PAGES_DEV = 2
N_SEQ = 128


def draw_tokens(key, part):
    key_base = jax.random.fold_in(key, 0)
    base_draw = jax.random.normal(key_base, (TOKENS, D), jnp.float32)
    return jnp.clip(base_draw, -6.0, 6.0).astype(jnp.bfloat16)


def shared_query(key):
    return jax.random.normal(jax.random.fold_in(key, 11), (D, HEADS * HD), jnp.float32) * D ** (-0.5)


def draw_w_query(key, part):
    return jnp.clip(shared_query(key), -1.0, 1.0).astype(jnp.bfloat16)


def draw_w_key(key, part):
    result = jax.random.normal(jax.random.fold_in(key, 12), (D, KVH * HD), jnp.float32) * D ** (-0.5)
    return jnp.clip(result, -4.0, 4.0).astype(jnp.bfloat16)


def draw_segment_ids(key, part):
    key_lengths, key_block_one, key_block_two, key_offset_one, key_offset_two = jax.random.split(key, 5)
    position = jnp.arange(TOKENS, dtype=jnp.int32)
    lengths = jax.random.randint(key_lengths, (TOKENS,), 1, 2 * SHORT, dtype=jnp.int32)
    starts = jnp.cumsum(lengths) - lengths
    flags = jnp.zeros((TOKENS,), jnp.int32).at[starts].set(1, mode='drop')
    half_blocks = TOKENS // BLOCK // 2
    block_keys = (key_block_one, key_block_two)
    offset_keys = (key_offset_one, key_offset_two)
    for which in range(2):
        first_block = jax.random.randint(block_keys[which], (), 0, half_blocks - REACH, dtype=jnp.int32) + which * half_blocks
        begin = first_block * BLOCK + jax.random.randint(offset_keys[which], (), 1, BLOCK, dtype=jnp.int32)
        inside = (position >= begin) & (position < begin + LONGSEG)
        flags = jnp.where(inside, 0, flags)
        flags = jnp.where((position == begin) | (position == begin + LONGSEG), 1, flags)
    flags = flags.at[0].set(1)
    flags = flags.at[TOKENS - 1].set(1)
    marked = jnp.where(flags > 0, position, 0)
    return lax.cummax(marked, axis=0).astype(jnp.int32)


def draw_page_table(key, part):
    block_keys = jax.random.split(key, PAGES // PAGES_DEV)
    orders = jax.vmap(lambda single: jax.random.permutation(single, PAGES_DEV))(block_keys)
    return orders.reshape(PAGES).astype(jnp.int32)


def block_levels(key, extent, shards, least, top_value):
    loudness, own = 1.0, jax.random.fold_in(key, 6)
    for dim, shards_of in shards:
        steps = jnp.exp(jax.random.uniform(jax.random.fold_in(own, dim), (shards_of,), jnp.float32, least / len(shards), top_value / len(shards)))
        loudness = loudness * jnp.repeat(steps, extent[dim] // shards_of).reshape([-1 if axis == dim else 1 for axis in range(len(extent))])
    return loudness


def normal_values(key, dims, width, most, cuts=(), kind=jnp.bfloat16):
    level = block_levels(key, dims, cuts, -0.22, 0.18) if cuts else 1.0
    entries = jax.random.normal(key, dims, jnp.float32) * width * level
    return jnp.minimum(jnp.maximum(entries, -most), most).astype(kind)


def setup_inputs(seed: int = 0) -> dict:
    seeds = jax.random.split(jax.random.key(seed), 9)
    return {
        "tokens": draw_tokens(jax.random.fold_in(seeds[8], 71), 0),
        "gain": jnp.clip(1.0 + 0.15 * jax.random.normal(seeds[1], (D,), jnp.float32), 0.25, 1.75),
        "w_query": draw_w_query(jax.random.fold_in(seeds[8], 71), 0),
        "w_key": draw_w_key(jax.random.fold_in(seeds[8], 71), 0),
        "w_value": normal_values(seeds[4], (D, KVH * HD), D ** -0.5, 0.09375, ((1, 2),)),
        "w_out": normal_values(seeds[5], (HEADS * HD, D), (HEADS * HD) ** -0.5, 0.09375, ((0, 2),)),
        "segment_ids": draw_segment_ids(jax.random.fold_in(seeds[8], 71), 0),
        "page_table": draw_page_table(jax.random.fold_in(seeds[8], 71), 0),
    }


norm_eps = 1e-05

def head_attention(query_head, key_blocks, value_blocks, masks, live):
    block_count = key_blocks.shape[0]
    key_width = key_blocks.shape[1]
    score_scale = query_head.shape[-1] ** (-0.5)
    query_wide = query_head.astype(jnp.float32)

    def block_scores(distance):
        scores = jnp.einsum('qgd,kd->gqk', query_wide, key_blocks[distance].astype(jnp.float32)) * score_scale
        return jnp.where(masks[distance][None], scores, -jnp.inf)

    def empty_scores():
        return jnp.full((query_head.shape[1], query_head.shape[0], key_width), -jnp.inf, jnp.float32)
    pieces = [block_scores(0)]
    for distance in range(1, block_count):
        pieces.append(lax.cond(live[distance], lambda: block_scores(distance), empty_scores))
    scores = jnp.concatenate(pieces, axis=2)
    row_peak = lax.optimization_barrier(jnp.max(scores, axis=2, keepdims=True))
    weights = jnp.exp(scores - row_peak).astype(jnp.bfloat16)
    weights_wide = weights.astype(jnp.float32)
    row_total = lax.optimization_barrier(jnp.sum(weights_wide, axis=2))
    all_values = value_blocks.reshape(block_count * key_width, value_blocks.shape[-1]).astype(jnp.float32)
    weighted = jnp.einsum('gqk,kd->qgd', weights_wide, all_values)
    return (weighted / row_total.T[:, :, None]).astype(jnp.bfloat16)

def reference(tokens, gain, w_query, w_key, w_value, w_out, segment_ids, page_table):
    wide_rows = tokens.astype(jnp.float32)
    normed = (wide_rows * lax.rsqrt(lax.optimization_barrier(jnp.mean(wide_rows * wide_rows, axis=1, keepdims=True)) + norm_eps) * gain).astype(jnp.bfloat16)
    query = jnp.dot(normed, w_query, preferred_element_type=jnp.float32).astype(jnp.bfloat16)
    key_rows = jnp.dot(normed, w_key, preferred_element_type=jnp.float32).astype(jnp.bfloat16)
    value_rows = jnp.dot(normed, w_value, preferred_element_type=jnp.float32).astype(jnp.bfloat16)
    pair_rows = jnp.stack([key_rows, value_rows], axis=0)
    pages = pair_rows.reshape(2, PAGES, PAGE, KVH, HD).transpose(1, 0, 3, 2, 4)
    slots = jnp.arange(PAGES, dtype=jnp.int32) // PAGES_DEV * PAGES_DEV + page_table.astype(jnp.int32)
    page_pool = jnp.zeros_like(pages).at[slots].set(pages)
    group_size = HEADS // KVH
    query_blocks = query.reshape(N_SEQ, BLOCK, KVH, group_size, HD)
    key_blocks = key_rows.reshape(N_SEQ, BLOCK, KVH, HD)
    value_blocks = value_rows.reshape(N_SEQ, BLOCK, KVH, HD)
    lower = jnp.arange(BLOCK)[None, :] <= jnp.arange(BLOCK)[:, None]

    def one_block(index):
        query_here = query_blocks[index]
        query_segs = lax.dynamic_slice_in_dim(segment_ids, (index * BLOCK).astype(jnp.int32), BLOCK)
        key_list, value_list, mask_list, live_list = ([], [], [], [])
        for distance in range(REACH + 1):
            source = jnp.maximum(index - distance, 0).astype(jnp.int32)
            valid = index - distance >= 0
            key_list.append(key_blocks[source])
            value_list.append(value_blocks[source])
            key_segs = lax.dynamic_slice_in_dim(segment_ids, (source * BLOCK).astype(jnp.int32), BLOCK)
            same = (key_segs[None, :] == query_segs[:, None]) & valid
            if distance == 0:
                same = same & lower
                live_list.append(jnp.array(True))
            else:
                live_list.append(valid & (key_segs[BLOCK - 1] == query_segs[0]))
            mask_list.append(same)
        masks = jnp.stack(mask_list)
        live = jnp.stack(live_list)
        keys_all = jnp.stack(key_list).transpose(2, 0, 1, 3)
        values_all = jnp.stack(value_list).transpose(2, 0, 1, 3)

        def per_head(inputs):
            return head_attention(inputs[0], inputs[1], inputs[2], masks, live)
        heads_out = lax.map(per_head, (query_here.transpose(1, 0, 2, 3), keys_all, values_all))
        return heads_out.transpose(1, 0, 2, 3).reshape(BLOCK, HEADS * HD)
    attention = lax.map(one_block, jnp.arange(N_SEQ, dtype=jnp.int32)).reshape(TOKENS, HEADS * HD)
    branch = jnp.dot(attention, w_out, preferred_element_type=jnp.float32)
    attn_out = branch.astype(jnp.bfloat16)
    mixed = (wide_rows + branch).astype(jnp.bfloat16)
    return (mixed, attn_out, page_pool)
```

```python
import functools

import jax
import jax.numpy as jnp
from jax import lax
from jax.experimental import pallas as pl
from jax.experimental.pallas import tpu as pltpu
from jax.sharding import PartitionSpec as P

HD = 128
EPS = 1e-05
NEG = -1e30
REACH = 8
ROW = 4
C = 2
MESH = pl.DeviceIdType.MESH


def kernel(
    n_seq,
    tok_hbm, gain_ref, wq_hbm, wk_hbm, wv_hbm, wo_hbm, seg_ref,
    mixed_hbm, attn_hbm, pages_hbm,
    X, N, W, B, Q, ACC, L, M, MB, QS, A, PP, PR, O1, O2,
    wsem, tsem, txs, txr, ss, rs, ps, pr, osem, gsem,
):
    kv = lax.axis_index("kv")
    s = lax.axis_index("seq")
    other = 1 - kv
    x = lax.rem(s, ROW)
    base = s - x
    right = base + lax.rem(x + 1, ROW)
    left = base + lax.rem(x + ROW - 1, ROW)
    up = lax.rem(s + ROW, n_seq)
    down = lax.rem(s + n_seq - ROW, n_seq)
    f32, bf16 = jnp.float32, jnp.bfloat16

    def load(slot, src, sem):
        return pltpu.make_async_copy(src, W.at[slot], wsem.at[sem])

    loads = []
    for h in range(2):
        loads.append(load(h, wk_hbm.at[pl.ds(h * 2048, 2048), :], h))
    for h in range(2):
        loads.append(load(2 + h, wv_hbm.at[pl.ds(h * 2048, 2048), :], 2 + h))
    for c in range(4):
        for h in range(2):
            i = 4 + 2 * c + h
            loads.append(load(i, wq_hbm.at[pl.ds(h * 2048, 2048), pl.ds(c * 512, 512)], i))
    own_tok = pltpu.make_async_copy(tok_hbm, X.at[kv], tsem)
    own_tok.start()
    for cp in loads[:4]:
        cp.start()

    barrier = pltpu.get_barrier_semaphore()
    pl.semaphore_signal(barrier, inc=1, device_id={"kv": other, "seq": s}, device_id_type=MESH)
    for peer in (right, left, up, down):
        pl.semaphore_signal(barrier, inc=1, device_id={"kv": kv, "seq": peer}, device_id_type=MESH)
    pl.semaphore_wait(barrier, 5)

    swap = pltpu.make_async_remote_copy(
        src_ref=tok_hbm, dst_ref=X.at[kv], send_sem=txs, recv_sem=txr,
        device_id={"kv": other, "seq": s}, device_id_type=MESH,
    )
    swap.start()
    for cp in loads[4:]:
        cp.start()

    for r in range(2):
        row = seg_ref[pl.ds(2 * s + r, 1), :].astype(f32)
        QS[pl.ds(r * 128, 128), :] = jnp.broadcast_to(row, (128, 128)).T

    gain = gain_ref[...]

    def norm_half(h):
        def body(i, carry):
            v = X[h, pl.ds(i * 16, 16), :].astype(f32)
            ms = jnp.mean(v * v, axis=1, keepdims=True)
            N[pl.ds(h * 128 + i * 16, 16), :] = (v * lax.rsqrt(ms + EPS) * gain).astype(bf16)
            return carry

        lax.fori_loop(0, 8, body, 0)

    own_tok.wait()
    norm_half(kv)
    swap.wait_recv()
    norm_half(other)

    def project(slot):
        return (
            jnp.dot(N[:, 0:2048], W[slot], preferred_element_type=f32)
            + jnp.dot(N[:, 2048:4096], W[slot + 1], preferred_element_type=f32)
        ).astype(bf16)

    loads[0].wait()
    loads[1].wait()
    B[0, 0] = project(0)
    loads[2].wait()
    loads[3].wait()
    B[0, 1] = project(2)
    outs = [load(n, wo_hbm.at[:, pl.ds(n * 512, 512)], 12 + n) for n in range(8)]
    for n in range(4):
        outs[n].start()

    def item(idx, c, src, dst, peer):
        rows = pl.ds(c * (256 // C), 256 // C)
        return pltpu.make_async_remote_copy(
            src_ref=B.at[src, :, rows, :], dst_ref=B.at[dst, :, rows, :],
            send_sem=ss.at[idx, c], recv_sem=rs.at[dst, c],
            device_id={"kv": kv, "seq": peer}, device_id_type=MESH,
        )

    last = x == ROW - 1
    first = x == 0
    zero = x * 0

    def y1(c):
        return item(0, c, 0, 4, up)

    def y2(c):
        return item(1, c, 4, 8, up)

    def xp1(c):
        return item(2, c, jnp.where(last, 4, 0), 1, right)

    def xp5(c):
        return item(3, c, jnp.where(last, 8, 4), 5, right)

    def xp2(c):
        return item(4, c, jnp.where(last, 5, 1), 2, right)

    def xm3(c):
        return item(5, c, jnp.where(first, 0, 4), 3, left)

    def xm7(c):
        return item(6, c, jnp.where(first, 4, 8), 7, left)

    def xm6(c):
        return item(7, c, jnp.where(first, 3, 7), 6, left)

    arrive = {1: xp1, 2: xp2, 3: xm3, 4: y1, 5: xp5, 6: xm6, 7: xm7, 8: y2}

    def wait_arrival(d, c):
        arrive[d](c).wait_recv()

    rows_i = lax.broadcasted_iota(jnp.int32, (256, 128), 0)
    cols_i = lax.broadcasted_iota(jnp.int32, (256, 128), 1)

    def attend(d):
        sd = lax.rem(s + n_seq - d, n_seq)
        for r in range(2):
            krow = seg_ref[pl.ds(2 * sd + r, 1), :].astype(f32)
            krow = jnp.where(s >= d, krow, -1.0)
            same = QS[...] == krow
            if d == 0:
                same = same & (cols_i + r * 128 <= rows_i)
            MB[:, r * 128:(r + 1) * 128] = jnp.where(same, 0.0, NEG)

        def body(g, carry):
            lanes = pl.ds(pl.multiple_of(g * 128, 128), 128)
            k = B[d, 0, :, lanes]
            va = jnp.concatenate([B[d, 1, :, lanes], jnp.ones((256, 128), bf16)], axis=1)
            for h in range(4):
                rows = pl.ds(h * 256, 256)
                sc = lax.dot_general(
                    Q[g, rows, :], k, (((1,), (1,)), ((), ())), preferred_element_type=f32
                ) * (HD ** -0.5) + MB[...]
                top = jnp.max(sc, axis=1, keepdims=True)
                if d == 0:
                    w = jnp.exp(sc - top).astype(bf16)
                    pv = jnp.dot(w, va, preferred_element_type=f32)
                    M[g, rows, :] = jnp.broadcast_to(top, (256, 128))
                    ACC[g, rows, :] = pv[:, :128]
                    L[g, rows, :] = pv[:, 128:]
                else:
                    old = M[g, rows, :]
                    new = jnp.maximum(old, jnp.broadcast_to(top, (256, 128)))
                    w = jnp.exp(sc - jnp.concatenate([new, new], axis=1)).astype(bf16)
                    pv = jnp.dot(w, va, preferred_element_type=f32)
                    fade = jnp.exp(old - new)
                    M[g, rows, :] = new
                    ACC[g, rows, :] = ACC[g, rows, :] * fade + pv[:, :128]
                    L[g, rows, :] = L[g, rows, :] * fade + pv[:, 128:]
            return carry

        lax.fori_loop(0, 4, body, 0)

    def query(c):
        loads[4 + 2 * c].wait()
        loads[5 + 2 * c].wait()
        q = project(4 + 2 * c)
        for h in range(4):
            Q[c, h * 256:(h + 1) * 256, :] = q[:, h * 128:(h + 1) * 128]

    for c in range(C):
        y1(c).start()

    @pl.when(x < ROW - 1)
    def _():
        for c in range(C):
            xp1(c).start()

    @pl.when(first)
    def _():
        for c in range(C):
            xm3(c).start()

    page_copies = []
    for p in range(2):
        for t in range(2):
            for g in range(4):
                i = (p * 2 + t) * 4 + g
                page_copies.append(pltpu.make_async_copy(
                    B.at[0, t, pl.ds(p * 128, 128), pl.ds(g * 128, 128)],
                    pages_hbm.at[p, t, g], gsem.at[i]))
    for cp in page_copies:
        cp.start()

    query(0)
    query(1)
    for n in range(4, 8):
        outs[n].start()
    for c in range(C):
        wait_arrival(4, c)
        y2(c).start()

        @pl.when(last)
        def _():
            xp1(c).start()

        @pl.when(x > 0)
        def _():
            xm3(c).start()

        if c == 0:
            query(2)

    @pl.when(x < ROW - 1)
    def _():
        for c in range(C):
            xp5(c).start()

    @pl.when(first)
    def _():
        for c in range(C):
            xm7(c).start()

    query(3)
    attend(0)
    for c in range(C):
        wait_arrival(1, c)
    for c in range(C):
        wait_arrival(3, c)
    attend(4)

    for c in range(C):
        wait_arrival(8, c)

        @pl.when(last)
        def _():
            xp5(c).start()

        @pl.when(x > 0)
        def _():
            xm7(c).start()

    @pl.when(x < ROW - 1)
    def _():
        for c in range(C):
            xp2(c).start()

    @pl.when(first)
    def _():
        for c in range(C):
            xm6(c).start()

    attend(1)
    for c in range(C):
        wait_arrival(5, c)

        @pl.when(last)
        def _():
            xp2(c).start()

        wait_arrival(7, c)

        @pl.when(x > 0)
        def _():
            xm6(c).start()

    attend(3)
    attend(8)
    attend(5)
    attend(7)
    for c in range(C):
        wait_arrival(2, c)
    attend(2)
    for c in range(C):
        wait_arrival(6, c)
    attend(6)

    for g in range(4):
        for h in range(4):
            rows = pl.ds(h * 256, 256)
            i = (g * 4 + h) * 128
            A[:, i:i + 128] = (ACC[g, rows, :] / L[g, rows, :]).astype(bf16)

    def give(n):
        return pltpu.make_async_remote_copy(
            src_ref=PP.at[n, other], dst_ref=PR.at[n], send_sem=ps.at[n], recv_sem=pr.at[n],
            device_id={"kv": other, "seq": s}, device_id_type=MESH,
        )

    def put(n):
        cols = pl.ds(n * 512, 512)
        return (
            pltpu.make_async_copy(O1.at[:, cols], attn_hbm.at[:, cols], osem.at[0, n]),
            pltpu.make_async_copy(O2.at[:, cols], mixed_hbm.at[:, cols], osem.at[1, n]),
        )

    def finish(n):
        give(n).wait_recv()
        cols = pl.ds(n * 512, 512)
        y = PP[n, kv] + PR[n]
        O1[:, cols] = y.astype(bf16)
        O2[:, cols] = (X[kv, :, cols].astype(f32) + y).astype(bf16)
        for cp in put(n):
            cp.start()

    for n in range(8):
        outs[n].wait()
        part = jnp.dot(A[...], W[n], preferred_element_type=f32)
        PP[n, 0] = part[:128]
        PP[n, 1] = part[128:]
        give(n).start()
        if n >= 2:
            finish(n - 2)
    finish(6)
    finish(7)

    swap.wait_send()
    for c in range(C):
        for f in arrive.values():
            f(c).wait_send()
    for n in range(8):
        give(n).wait_send()
        for cp in put(n):
            cp.wait()
    for cp in page_copies:
        cp.wait()


def shards(n_seq, tokens, gain, w_query, w_key, w_value, w_out, segment_ids, page_table):
    bf16, f32 = jnp.bfloat16, jnp.float32
    any_spec = pl.BlockSpec(memory_space=pl.ANY)
    vmem_spec = pl.BlockSpec(memory_space=pltpu.VMEM)
    dma = pltpu.SemaphoreType.DMA
    mixed, attn_out, pages = pl.pallas_call(
        functools.partial(kernel, n_seq),
        out_shape=(
            jax.ShapeDtypeStruct((128, 4096), bf16),
            jax.ShapeDtypeStruct((128, 4096), bf16),
            jax.ShapeDtypeStruct((2, 2, 4, 128, 128), bf16),
        ),
        in_specs=[any_spec, vmem_spec, any_spec, any_spec, any_spec, any_spec, vmem_spec],
        out_specs=(any_spec, any_spec, any_spec),
        scratch_shapes=[
            pltpu.VMEM((2, 128, 4096), bf16),
            pltpu.VMEM((256, 4096), bf16),
            pltpu.VMEM((12, 2048, 512), bf16),
            pltpu.VMEM((REACH + 1, 2, 256, 512), bf16),
            pltpu.VMEM((4, 1024, 128), bf16),
            pltpu.VMEM((4, 1024, 128), f32),
            pltpu.VMEM((4, 1024, 128), f32),
            pltpu.VMEM((4, 1024, 128), f32),
            pltpu.VMEM((256, 256), f32),
            pltpu.VMEM((256, 128), f32),
            pltpu.VMEM((256, 2048), bf16),
            pltpu.VMEM((8, 2, 128, 512), f32),
            pltpu.VMEM((8, 128, 512), f32),
            pltpu.VMEM((128, 4096), bf16),
            pltpu.VMEM((128, 4096), bf16),
            dma((20,)), dma, dma, dma,
            dma((8, C)), dma((REACH + 1, C)),
            dma((8,)), dma((8,)), dma((2, 8)), dma((16,)),
        ],
        compiler_params=pltpu.CompilerParams(
            collective_id=0, has_side_effects=True, vmem_limit_bytes=60 * 1024 * 1024
        ),
    )(tokens, gain.reshape(1, 4096), w_query, w_key, w_value, w_out, segment_ids.reshape(256, 128))
    page_pool = jnp.where(page_table[0] == 0, pages, pages[::-1])
    return mixed, attn_out, page_pool


def solution(mesh):
    in_specs = (
        P(("seq", "kv"), None),
        P(),
        P(None, "kv"),
        P(None, "kv"),
        P(None, "kv"),
        P("kv", None),
        P(),
        P("seq"),
    )
    out_specs = (P(("seq", "kv"), None), P(("seq", "kv"), None), P("seq", None, "kv", None, None))
    return jax.shard_map(
        functools.partial(shards, mesh.shape["seq"]),
        mesh=mesh, in_specs=in_specs, out_specs=out_specs, check_vma=False,
    )
```

```python
import functools

import jax
import jax.numpy as jnp
from jax import lax
from jax.experimental import pallas as pl
from jax.experimental.pallas import tpu as pltpu
from jax.sharding import PartitionSpec as P

HD = 128
EPS = 1e-05
NEG = -1e30
REACH = 8
ROW = 4
MESH = pl.DeviceIdType.MESH


def kernel(
    n_seq,
    tok_hbm, gain_ref, wq_hbm, wk_hbm, wv_hbm, wo_hbm, seg_ref,
    mixed_ref, attn_ref, pages_ref,
    X, N, W, B, Q, ACC, L, M, MB, QS, QA, KA, PP, PR,
    wsem, tsem, txs, txr, ss, rs, ps, pr, gsem,
):
    kv = lax.axis_index("kv")
    s = lax.axis_index("seq")
    other = 1 - kv
    x = lax.rem(s, ROW)
    base = s - x
    right = base + lax.rem(x + 1, ROW)
    left = base + lax.rem(x + ROW - 1, ROW)
    up = lax.rem(s + ROW, n_seq)
    down = lax.rem(s + n_seq - ROW, n_seq)
    first = x == 0
    last = x == ROW - 1
    f32, bf16 = jnp.float32, jnp.bfloat16

    def load(i, src):
        return pltpu.make_async_copy(src, W.at[i], wsem.at[i])

    loads = []
    for w_hbm in (wk_hbm, wv_hbm):
        for h in range(2):
            loads.append(load(len(loads), w_hbm.at[pl.ds(h * 2048, 2048), :]))
    for c in range(4):
        for h in range(2):
            loads.append(load(
                len(loads), wq_hbm.at[pl.ds(h * 2048, 2048), pl.ds(c * 512, 512)]))

    def load_out(g, n):
        return pltpu.make_async_copy(
            wo_hbm.at[pl.ds(g * 512, 512), pl.ds(n * 512, 512)],
            W.at[2 * g + n // 4, pl.ds((n % 4) * 512, 512), :],
            wsem.at[12 + g * 8 + n])

    own_tok = pltpu.make_async_copy(tok_hbm, X.at[kv], tsem)
    own_tok.start()
    for cp in loads[:4]:
        cp.start()

    barrier = pltpu.get_barrier_semaphore()
    pl.semaphore_signal(barrier, inc=1, device_id={"kv": other, "seq": s}, device_id_type=MESH)
    for peer in (right, left, up, down):
        pl.semaphore_signal(barrier, inc=1, device_id={"kv": kv, "seq": peer}, device_id_type=MESH)
    pl.semaphore_wait(barrier, 5)

    swap = pltpu.make_async_remote_copy(
        src_ref=tok_hbm, dst_ref=X.at[kv], send_sem=txs, recv_sem=txr,
        device_id={"kv": other, "seq": s}, device_id_type=MESH,
    )
    swap.start()
    for cp in loads[4:]:
        cp.start()

    def clear(n, carry):
        PP[n] = jnp.zeros((2, 128, 512), f32)
        return carry

    lax.fori_loop(0, 8, clear, 0)
    gain = gain_ref[...]

    def norm_half(h):
        def body(i, carry):
            v = X[h, pl.ds(i * 16, 16), :].astype(f32)
            ms = jnp.mean(v * v, axis=1, keepdims=True)
            N[pl.ds(h * 128 + i * 16, 16), :] = (v * lax.rsqrt(ms + EPS) * gain).astype(bf16)
            return carry

        lax.fori_loop(0, 8, body, 0)

    own_tok.wait()
    norm_half(kv)

    def column(block, r):
        row = seg_ref[pl.ds(2 * block + r, 1), :].astype(f32)
        return jnp.broadcast_to(row, (128, 128)).T

    lane = lax.broadcasted_iota(jnp.int32, (128, 128), 1)
    opening = seg_ref[pl.ds(2 * s, 1), :].astype(f32)[:, :1]
    for r in range(2):
        rows = pl.ds(r * 128, 128)
        own = column(s, r)
        QS[rows, :] = own
        out = jnp.where(own == opening, 0.0, NEG)
        QA[rows, :] = jnp.where(lane == 0, out, jnp.where(lane == 1, 1.0, 0.0)).astype(bf16)

    def key_mask(d, carry):
        block = lax.rem(s + n_seq - d, n_seq)
        for r in range(2):
            out = jnp.where((column(block, r) == opening) & (s >= d), 0.0, NEG)
            KA[d, pl.ds(r * 128, 128), :] = jnp.where(
                lane == 1, out, jnp.where(lane == 0, 1.0, 0.0)).astype(bf16)
        return carry

    lax.fori_loop(1, REACH + 1, key_mask, 0)
    swap.wait_recv()
    norm_half(other)

    def project(slot):
        return (
            jnp.dot(N[:, 0:2048], W[slot], preferred_element_type=f32)
            + jnp.dot(N[:, 2048:4096], W[slot + 1], preferred_element_type=f32)
        ).astype(bf16)

    for t in range(2):
        loads[2 * t].wait()
        loads[2 * t + 1].wait()
        rows = project(2 * t)
        for g in range(4):
            B[0, g, t] = rows[:, g * 128:(g + 1) * 128]

    def item(idx, g, src, dst, peer):
        return pltpu.make_async_remote_copy(
            src_ref=B.at[src, g], dst_ref=B.at[dst, g],
            send_sem=ss.at[idx, g], recv_sem=rs.at[dst, g],
            device_id={"kv": kv, "seq": peer}, device_id_type=MESH,
        )

    def y4(g):
        return item(0, g, 0, 4, up)

    def y8(g):
        return item(1, g, 4, 8, up)

    def x1(g):
        return item(2, g, jnp.where(last, 4, 0), 1, right)

    def x5(g):
        return item(3, g, jnp.where(last, 8, 4), 5, right)

    def y5(g):
        return item(3, g, 1, 5, up)

    def x2(g):
        return item(4, g, jnp.where(last, 5, 1), 2, right)

    def x3(g):
        return item(5, g, jnp.where(first, 0, 4), 3, left)

    def x7(g):
        return item(6, g, jnp.where(first, 4, 8), 7, left)

    def x6(g):
        return item(7, g, jnp.where(first, 3, 7), 6, left)

    def y6(g):
        return item(7, g, 2, 6, up)

    relay = {1: x1, 2: x2, 3: x3, 4: y4, 5: x5, 6: x6, 7: x7, 8: y8}

    def arrived(d, g):
        relay[d](g).wait_recv()

    def send(cond, d, g):
        @pl.when(cond)
        def _():
            relay[d](g).start()

    for g in range(4):
        y4(g).start()
        send(x < ROW - 1, 1, g)
        send(first, 3, g)

    page_copies = []
    for p in range(2):
        for t in range(2):
            for g in range(4):
                page_copies.append(pltpu.make_async_copy(
                    B.at[0, g, t, pl.ds(p * 128, 128), :], pages_ref.at[p, t, g],
                    gsem.at[len(page_copies)]))
    for cp in page_copies:
        cp.start()

    def start_out(g):
        for n in range(8):
            load_out(g, n).start()

    def query(c):
        loads[4 + 2 * c].wait()
        loads[5 + 2 * c].wait()
        q = project(4 + 2 * c)
        for h in range(4):
            Q[c, h * 256:(h + 1) * 256, :] = q[:, h * 128:(h + 1) * 128]

    unit = HD ** -0.5 * 1.4426950408889634
    over = (((1,), (1,)), ((), ()))
    ones = jnp.ones((256, 128), bf16)

    def wide(v, n):
        return jnp.concatenate([v] * n, axis=1)

    def own_mask():
        rows_i = lax.broadcasted_iota(jnp.int32, (256, 128), 0)
        cols_i = lax.broadcasted_iota(jnp.int32, (256, 128), 1)
        for r in range(2):
            krow = seg_ref[pl.ds(2 * s + r, 1), :].astype(f32)
            same = (QS[...] == krow) & (cols_i + r * 128 <= rows_i)
            MB[:, r * 128:(r + 1) * 128] = jnp.where(same, 0.0, NEG)

    def attend_own(g):
        va = jnp.concatenate([B[0, g, 1], ones], axis=1)
        for h in range(4):
            rows = pl.ds(h * 256, 256)
            sc = lax.dot_general(
                Q[g, rows, :], B[0, g, 0], over, preferred_element_type=f32
            ) * unit + MB[...]
            top = jnp.broadcast_to(jnp.max(sc, axis=1, keepdims=True), (256, 128))
            w = jnp.exp2(sc - wide(top, 2)).astype(bf16)
            pv = jnp.dot(w, va, preferred_element_type=f32)
            M[g, rows, :] = top
            ACC[g, rows, :] = pv[:, :128]
            L[g, rows, :] = pv[:, 128:]

    def attend(d, e, g):
        k = jnp.concatenate([
            jnp.concatenate([B[d, g, 0], KA[d]], axis=1),
            jnp.concatenate([B[e, g, 0], KA[e]], axis=1)], axis=0)
        va = jnp.concatenate([
            jnp.concatenate([B[d, g, 1], ones], axis=1),
            jnp.concatenate([B[e, g, 1], ones], axis=1)], axis=0)
        for h in range(4):
            rows = pl.ds(h * 256, 256)
            q = jnp.concatenate([Q[g, rows, :], QA[...]], axis=1)
            sc = lax.dot_general(q, k, over, preferred_element_type=f32) * unit
            top = jnp.broadcast_to(jnp.max(sc, axis=1, keepdims=True), (256, 128))
            old = M[g, rows, :]
            new = jnp.maximum(old, top)
            w = jnp.exp2(sc - wide(new, 4)).astype(bf16)
            pv = jnp.dot(w, va, preferred_element_type=f32)
            fade = jnp.exp2(old - new)
            M[g, rows, :] = new
            ACC[g, rows, :] = ACC[g, rows, :] * fade + pv[:, :128]
            L[g, rows, :] = L[g, rows, :] * fade + pv[:, 128:]

    query(0)
    for g in range(4):
        arrived(4, g)
        y8(g).start()
        send(last, 1, g)
        send(x > 0, 3, g)
        if g < 3:
            send(x < ROW - 1, 5, g)
        send(first, 7, g)
        if g < 3:
            query(g + 1)
    for g in range(4):
        start_out(g)
    own_mask()
    def each_head(step):
        def body(g, carry):
            step(g)
            return carry

        lax.fori_loop(0, 4, body, 0)

    @each_head
    def _(g):
        arrived(1, g)
        send(x < ROW - 1, 2, g)

        @pl.when(g == 3)
        def _():
            y5(g).start()

        arrived(3, g)
        send(first & (g > 0), 6, g)
        attend_own(g)

    @each_head
    def _(g):
        arrived(8, g)
        send(last & (g < 3), 5, g)
        send(x > 0, 7, g)
        attend(4, 1, g)

    @each_head
    def _(g):
        arrived(5, g)
        send(last, 2, g)
        arrived(7, g)
        send((x > 0) & (g > 0), 6, g)
        attend(3, 8, g)

    @each_head
    def _(g):
        arrived(2, g)

        @pl.when(g == 0)
        def _():
            y6(g).start()

        attend(5, 7, g)

    def give(n):
        return pltpu.make_async_remote_copy(
            src_ref=PP.at[n, other], dst_ref=PR.at[n], send_sem=ps.at[n], recv_sem=pr.at[n],
            device_id={"kv": other, "seq": s}, device_id_type=MESH,
        )

    def finish(n):
        give(n).wait_recv()
        cols = pl.ds(n * 512, 512)
        y = PP[n, kv] + PR[n]
        attn_ref[:, cols] = y.astype(bf16)
        mixed_ref[:, cols] = (X[kv, :, cols].astype(f32) + y).astype(bf16)

    def head_out(g):
        return jnp.concatenate([
            (ACC[g, pl.ds(h * 256, 256), :] / L[g, pl.ds(h * 256, 256), :]).astype(bf16)
            for h in range(4)], axis=1)

    def head_part(a, g, n):
        load_out(g, n).wait()
        return jnp.dot(
            a, W[2 * g + n // 4, pl.ds((n % 4) * 512, 512), :], preferred_element_type=f32)

    def settle(i, carry):
        g = lax.rem(i + 1, 3)
        arrived(6, g)
        attend(2, 6, g)
        a = head_out(g)
        for n in range(8):
            part = head_part(a, g, n)
            for r in range(2):
                half = part[r * 128:(r + 1) * 128]
                PP[n, r] = PP[n, r] + half
        return carry

    lax.fori_loop(0, 3, settle, 0)
    arrived(6, 3)
    attend(2, 6, 3)
    a = head_out(3)
    for n in range(8):
        part = head_part(a, 3, n)
        for r in range(2):
            PP[n, r] = PP[n, r] + part[r * 128:(r + 1) * 128]
        give(n).start()
        if n >= 2:
            finish(n - 2)
    finish(6)
    finish(7)

    swap.wait_send()
    for g in range(4):
        for f in relay.values():
            f(g).wait_send()
    for n in range(8):
        give(n).wait_send()
    for cp in page_copies:
        cp.wait()


def shards(n_seq, tokens, gain, w_query, w_key, w_value, w_out, segment_ids, page_table):
    bf16, f32 = jnp.bfloat16, jnp.float32
    any_spec = pl.BlockSpec(memory_space=pl.ANY)
    vmem_spec = pl.BlockSpec(memory_space=pltpu.VMEM)
    dma = pltpu.SemaphoreType.DMA
    mixed, attn_out, pages = pl.pallas_call(
        functools.partial(kernel, n_seq),
        out_shape=(
            pltpu.VMEM((128, 4096), bf16),
            pltpu.VMEM((128, 4096), bf16),
            pltpu.VMEM((2, 2, 4, 128, 128), bf16),
        ),
        in_specs=[any_spec, vmem_spec, any_spec, any_spec, any_spec, any_spec, vmem_spec],
        out_specs=(vmem_spec, vmem_spec, vmem_spec),
        scratch_shapes=[
            pltpu.VMEM((2, 128, 4096), bf16),
            pltpu.VMEM((256, 4096), bf16),
            pltpu.VMEM((12, 2048, 512), bf16),
            pltpu.VMEM((REACH + 1, 4, 2, 256, 128), bf16),
            pltpu.VMEM((4, 1024, 128), bf16),
            pltpu.VMEM((4, 1024, 128), f32),
            pltpu.VMEM((4, 1024, 128), f32),
            pltpu.VMEM((4, 1024, 128), f32),
            pltpu.VMEM((256, 256), f32),
            pltpu.VMEM((256, 128), f32),
            pltpu.VMEM((256, 128), bf16),
            pltpu.VMEM((REACH + 1, 256, 128), bf16),
            pltpu.VMEM((8, 2, 128, 512), f32),
            pltpu.VMEM((8, 128, 512), f32),
            dma((44,)), dma, dma, dma,
            dma((8, 4)), dma((REACH + 1, 4)),
            dma((8,)), dma((8,)), dma((16,)),
        ],
        compiler_params=pltpu.CompilerParams(
            collective_id=0, has_side_effects=True, vmem_limit_bytes=56 * 1024 * 1024
        ),
    )(tokens, gain.reshape(1, 4096), w_query, w_key, w_value, w_out, segment_ids.reshape(256, 128))
    page_pool = jnp.where(page_table[0] == 0, pages, pages[::-1])
    return mixed, attn_out, page_pool


def solution(mesh):
    in_specs = (
        P(("seq", "kv"), None),
        P(),
        P(None, "kv"),
        P(None, "kv"),
        P(None, "kv"),
        P("kv", None),
        P(),
        P("seq"),
    )
    out_specs = (P(("seq", "kv"), None), P(("seq", "kv"), None), P("seq", None, "kv", None, None))
    return jax.shard_map(
        functools.partial(shards, mesh.shape["seq"]),
        mesh=mesh, in_specs=in_specs, out_specs=out_specs, check_vma=False,
    )
```
